32 devices in a mesh: gx: 4 (over x, core), gy: 2 (over y), gz: 4 (over z).
Axes of the slice: x: 2, y: 2, z: 4, core: 2. Of those that a mesh axis runs over, the one named last changes fastest.
Arguments:
- features: bfloat16 [4, 2, 4, 16, 3200], P('gx', 'gy', 'gz'), may hold values from -6 to 6
- box_atoms: int32 [4, 2, 4], P('gx', 'gy', 'gz'), may hold values from 5 to 16, as said below
- edge_count: int32 [4, 2, 4], P('gx', 'gy', 'gz'), may hold values from 85 to 256, as said below
- edge_tower: int32 [4, 2, 4, 256], P('gx', 'gy', 'gz'), may hold values from 0 to 47, as said below
- edge_plate: int32 [4, 2, 4, 256], P('gx', 'gy', 'gz'), may hold values from 0 to 143, as said below
- wigner: float32 [4, 2, 4, 115, 256], P('gx', 'gy', 'gz'), may hold values from -1 to 1, as said below
- radial: bfloat16 [4, 2, 4, 256, 128], P('gx', 'gy', 'gz'), may hold values from 0.049804688 to 0.5
- so2_zero: bfloat16 [640, 640], replicated, may hold values from -0.25 to 0.25
- so2_one: bfloat16 [2, 512, 512], replicated, may hold values from -0.1875 to 0.1875
- so2_two: bfloat16 [2, 384, 384], replicated, may hold values from -0.21875 to 0.21875
Outputs:
- updated: bfloat16 [4, 2, 4, 16, 3200], P('gx', 'gy', 'gz')
The draws below stay inside these ranges and needn't reach their ends.
Inputs may be any that keep to these rules, and one draw needn't show every extreme that they name: `box_atoms`: the fullest box holds exactly 16 atoms in every draw; counts span a factor of three. `edge_count`: some device holds exactly 256 live edges in every draw. `edge_tower`: every entry d * 16 + a names an atom a present in tower box d, in live and padded slots alike. `edge_plate`: every entry p * 16 + a names an atom a present in plate box p, in live and padded slots alike. `wigner`: for each edge and degree, the rows are rows of an orthogonal matrix.
All inputs are finite; a program needn't handle non-finite values.
Results may differ from the reference program's by a relative error of at most 0.007.
Values may be sent and summed in bfloat16 or wider, within the bound.
No kernel may reach another device: no remote copies, remote signals or barrier semaphores. Data moves between devices by JAX's collectives and lax.ppermute only.
A program may use at most 64 MiB of HBM per device.

```python
import math
import jax
import jax.numpy as jnp
from jax import lax

C = 128
DEGREE = 4
ORDER = 2
COEFS = 25
ATOMS = 16
EDGES = 256
BX = 4
BY = 2
BZ = 4


def atom_counts(key):
    lowest = max(1, ATOMS // 3)
    counts = jax.random.randint(jax.random.fold_in(key, 11), (BX, BY, BZ), lowest, ATOMS + 1)
    chosen = jax.random.randint(jax.random.fold_in(key, 12), (), 0, BX * BY * BZ)
    places = jnp.arange(BX * BY * BZ, dtype=jnp.int32).reshape(BX, BY, BZ)
    return jnp.where(places == chosen, ATOMS, counts).astype(jnp.int32)


def draw_box_atoms(key, part):
    return atom_counts(key)


def draw_edge_count(key, part):
    lowest = max(1, EDGES // 3)
    counts = jax.random.randint(jax.random.fold_in(key, 21), (BX, BY, BZ), lowest, EDGES + 1)
    chosen = jax.random.randint(jax.random.fold_in(key, 22), (), 0, BX * BY * BZ)
    places = jnp.arange(BX * BY * BZ, dtype=jnp.int32).reshape(BX, BY, BZ)
    return jnp.where(places == chosen, EDGES, counts).astype(jnp.int32)


def pick_atoms(key, neighbour_counts):
    slots = neighbour_counts.shape[0]
    which = jax.random.randint(jax.random.fold_in(key, 1), (BX, BY, BZ, EDGES), 0, slots)
    available = jnp.take_along_axis(jnp.moveaxis(neighbour_counts, 0, -1), which, axis=3)
    raw_bits = jax.random.randint(jax.random.fold_in(key, 2), (BX, BY, BZ, EDGES), 0, 1 << 20)
    return (which * ATOMS + raw_bits % available).astype(jnp.int32)


def draw_edge_tower(key, part):
    counts = atom_counts(key)
    beside_all = jnp.stack([jnp.roll(counts, -step_x, axis=0) for step_x in (-1, 0, 1)])
    return pick_atoms(jax.random.fold_in(key, 31), beside_all)


def draw_edge_plate(key, part):
    counts = atom_counts(key)
    beside_all = jnp.stack([jnp.roll(jnp.roll(counts, -step_y, axis=1), -step_z, axis=2) for step_y in (-1, 0, 1) for step_z in (-1, 0, 1)])
    return pick_atoms(jax.random.fold_in(key, 41), beside_all)


def draw_wigner(key, part):
    blocks = []
    for degree in range(DEGREE + 1):
        span_cols = 2 * degree + 1
        within = min(degree, ORDER)
        inner = jax.random.fold_in(key, 51 + degree)
        raw = jax.random.normal(inner, (BX, BY, BZ, EDGES, span_cols, span_cols), jnp.float32)
        raw = raw + 0.1 * jnp.eye(span_cols, dtype=jnp.float32)
        basis = jnp.linalg.qr(raw)[0]
        kept = basis[..., degree - within:degree + within + 1, :]
        kept = kept.reshape(BX, BY, BZ, EDGES, (2 * within + 1) * span_cols)
        blocks.append(jnp.moveaxis(kept, 3, 4))
    return jnp.concatenate(blocks, axis=3).astype(jnp.float32)


def block_levels(stream_key, extent, split, smallest, largest):
    loudness = 1.0
    for axis_at, shards_of in split:
        heights = jax.random.uniform(jax.random.fold_in(jax.random.fold_in(stream_key, 6), axis_at), (shards_of,), jnp.float32, smallest / len(split), largest / len(split))
        loudness = loudness * jnp.repeat(jnp.exp(heights), extent[axis_at] // shards_of).reshape((-1,) + (1,) * (len(extent) - 1 - axis_at))
    return loudness


def bell_draw(rng, extent, scale, most, cuts=(), kind=jnp.bfloat16):
    factor_of = block_levels(rng, extent, cuts, -0.22, 0.18) if cuts else 1.0
    drawn = jax.random.normal(rng, extent, jnp.float32) * scale * factor_of
    return jnp.minimum(jnp.maximum(drawn, -most), most).astype(kind)


def setup_inputs(seed: int = 0) -> dict:
    seeds = jax.random.split(jax.random.key(seed), 11)
    return {
        "features": bell_draw(seeds[0], (BX, BY, BZ, ATOMS, COEFS * C), 1.0, 6.0, ((0, 4), (1, 2), (2, 4))),
        "box_atoms": draw_box_atoms(jax.random.fold_in(seeds[10], 71), 0),
        "edge_count": draw_edge_count(jax.random.fold_in(seeds[10], 71), 0),
        "edge_tower": draw_edge_tower(jax.random.fold_in(seeds[10], 71), 0),
        "edge_plate": draw_edge_plate(jax.random.fold_in(seeds[10], 71), 0),
        "wigner": draw_wigner(jax.random.fold_in(seeds[10], 71), 0),
        "radial": jnp.clip(jnp.exp(math.log(0.5) - 2.306499 * jax.random.uniform(seeds[6], (BX, BY, BZ, EDGES, C), jnp.float32) ** block_levels(seeds[6], (BX, BY, BZ, EDGES, C), ((0, 4), (1, 2), (2, 4)), -0.2, 0.2)), 0.049804688, 0.5).astype(jnp.bfloat16),
        "so2_zero": bell_draw(seeds[7], ((DEGREE + 1) * C, (DEGREE + 1) * C), ((DEGREE + 1) * C) ** -0.5, 0.25),
        "so2_one": bell_draw(seeds[8], (2, DEGREE * C, DEGREE * C), (2 * DEGREE * C) ** -0.5, 0.1875),
        "so2_two": bell_draw(seeds[9], (2, (DEGREE - 1) * C, (DEGREE - 1) * C), (2 * (DEGREE - 1) * C) ** -0.5, 0.21875),
    }


def rotate_forward(edge_rows, wig):
    pieces = {}
    offset = 0
    for degree in range(DEGREE + 1):
        within = min(degree, ORDER)
        for azimuth in range(-within, within + 1):
            summed = jnp.zeros((edge_rows.shape[0], edge_rows.shape[2]), jnp.float32)
            for column in range(-degree, degree + 1):
                summed = summed + wig[offset][:, None] * edge_rows[:, degree * degree + degree + column, :]
                offset += 1
            pieces[degree, azimuth] = summed
    return pieces

def rotate_back(pieces, wig):
    blocks = []
    offset = 0
    for degree in range(DEGREE + 1):
        within = min(degree, ORDER)
        span_cols = 2 * degree + 1
        summed = [None] * span_cols
        for azimuth in range(-within, within + 1):
            for column in range(span_cols):
                product = wig[offset][:, None] * pieces[degree, azimuth]
                summed[column] = product if summed[column] is None else summed[column] + product
                offset += 1
        blocks.extend(summed)
    return jnp.stack(blocks, axis=1)

def mix_orders(pieces, gate, so2_zero, so2_one, so2_two):
    channels = gate.shape[1]

    def lowered(degree, azimuth):
        return (pieces[degree, azimuth] * gate).astype(jnp.bfloat16)
    result = {}
    zeroth = jnp.concatenate([lowered(degree, 0) for degree in range(DEGREE + 1)], axis=1)
    mixed = jnp.dot(zeroth.astype(jnp.float32), so2_zero.astype(jnp.float32), preferred_element_type=jnp.float32)
    for degree in range(DEGREE + 1):
        result[degree, 0] = mixed[:, degree * channels:(degree + 1) * channels]
    for azimuth, table in ((1, so2_one), (2, so2_two)):
        degrees = list(range(azimuth, DEGREE + 1))
        plus = jnp.concatenate([lowered(degree, azimuth) for degree in degrees], axis=1)
        minus = jnp.concatenate([lowered(degree, -azimuth) for degree in degrees], axis=1)
        real_part = jnp.dot(plus.astype(jnp.float32), table[0].astype(jnp.float32), preferred_element_type=jnp.float32) - jnp.dot(minus.astype(jnp.float32), table[1].astype(jnp.float32), preferred_element_type=jnp.float32)
        imag_part = jnp.dot(plus.astype(jnp.float32), table[1].astype(jnp.float32), preferred_element_type=jnp.float32) + jnp.dot(minus.astype(jnp.float32), table[0].astype(jnp.float32), preferred_element_type=jnp.float32)
        for place, degree in enumerate(degrees):
            result[degree, azimuth] = real_part[:, place * channels:(place + 1) * channels]
            result[degree, -azimuth] = imag_part[:, place * channels:(place + 1) * channels]
    return result

def edge_message(source_rows, wig, gate, live, so2_zero, so2_one, so2_two):
    channels = gate.shape[1]
    shaped = source_rows.reshape(source_rows.shape[0], -1, channels)
    pieces = rotate_forward(shaped, wig)
    mixed = mix_orders(pieces, gate, so2_zero, so2_one, so2_two)
    message = rotate_back(mixed, wig).reshape(source_rows.shape[0], -1)
    return jnp.where(live[:, None], message, 0.0).astype(jnp.bfloat16)

def reference(features, box_atoms, edge_count, edge_tower, edge_plate, wigner, radial, so2_zero, so2_one, so2_two):
    span_x, span_y, span_z, atoms, feature_width = features.shape
    edges = edge_tower.shape[3]
    boxes = span_x * span_y * span_z
    flat_features = features.reshape(boxes * atoms, feature_width)
    tower_lists = edge_tower.reshape(boxes, edges)
    plate_lists = edge_plate.reshape(boxes, edges)
    counts = edge_count.reshape(boxes)
    rotations = wigner.reshape(boxes, wigner.shape[3], edges)
    gates = radial.reshape(boxes, edges, radial.shape[4])
    atom_ids = jnp.arange(atoms, dtype=jnp.int32)

    def device_step(summed, flat_index):
        box_x = flat_index // (span_y * span_z)
        box_y = flat_index // span_z % span_y
        box_z = flat_index % span_z
        tower_boxes = jnp.stack([(box_x + step_x) % span_x * span_y * span_z + box_y * span_z + box_z for step_x in (-1, 0, 1)])
        plate_boxes = jnp.stack([box_x * span_y * span_z + (box_y + step_y) % span_y * span_z + (box_z + step_z) % span_z for step_y in (-1, 0, 1) for step_z in (-1, 0, 1)])
        tower_atoms = (tower_boxes[:, None] * atoms + atom_ids[None, :]).reshape(-1).astype(jnp.int32)
        plate_atoms = (plate_boxes[:, None] * atoms + atom_ids[None, :]).reshape(-1).astype(jnp.int32)
        source_atom = tower_atoms[tower_lists[flat_index]]
        target_atom = plate_atoms[plate_lists[flat_index]]
        live = jnp.arange(edges, dtype=jnp.int32) < counts[flat_index]
        wig = rotations[flat_index]
        gate = gates[flat_index].astype(jnp.float32)
        to_plate = edge_message(flat_features[source_atom].astype(jnp.float32), wig, gate, live, so2_zero, so2_one, so2_two)
        to_tower = edge_message(flat_features[target_atom].astype(jnp.float32), wig, gate, live, so2_zero, so2_one, so2_two)
        summed = summed.at[target_atom].add(to_plate.astype(jnp.float32))
        summed = summed.at[source_atom].add(to_tower.astype(jnp.float32))
        return (summed, None)
    start = jnp.zeros((boxes * atoms, feature_width), jnp.float32)
    summed, unused = lax.scan(device_step, start, jnp.arange(boxes, dtype=jnp.int32))
    updated = flat_features.astype(jnp.float32) + summed
    updated = updated.reshape(span_x, span_y, span_z, atoms, feature_width)
    present = atom_ids[None, None, None, :] < box_atoms[..., None]
    return jnp.where(present[..., None], updated, 0.0).astype(jnp.bfloat16)
```

```python
import functools

import jax
import jax.numpy as jnp
from jax import lax
from jax.experimental import pallas as pl
from jax.experimental.pallas import tpu as pltpu
from jax.sharding import PartitionSpec as P

DEGREE = 4
ORDER = 2
COEFS = (DEGREE + 1) ** 2
LAST_LAST = (((1,), (1,)), ((), ()))
FIRST_FIRST = (((0,), (0,)), ((), ()))


def steps_of(axis):
    return (0, 1, -1)[: min(lax.axis_size(axis), 3)]


def place_of(axis):
    return [(0, 0, 0), (1, 0, 1), (2, 0, 1)][min(lax.axis_size(axis), 3) - 1]


def hand_on(block, axis, distance):
    count = lax.axis_size(axis)
    return lax.ppermute(block, axis, [(i, (i + distance) % count) for i in range(count)])


def entries():
    found = []
    for degree in range(DEGREE + 1):
        within = min(degree, ORDER)
        for azimuth in range(-within, within + 1):
            found += [(degree, azimuth, column) for column in range(2 * degree + 1)]
    return found


def offset_of(degree, azimuth):
    return entries().index((degree, azimuth, 0))


def whole(shape):
    return pl.BlockSpec(shape, lambda: (0,) * len(shape), memory_space=pltpu.VMEM)


def prepare_kernel(
    tower_classes, plate_classes, count, tower_ref, plate_ref, wigner, radial, zero, one, two,
    tower_pick, plate_pick, spread, gate, zero_t, one_t, two_t,
):
    edges = radial.shape[0]
    live = lax.broadcasted_iota(jnp.int32, (1, edges), 1) < count[0]
    for index_ref, classes, pick in (
        (tower_ref, tower_classes, tower_pick),
        (plate_ref, plate_classes, plate_pick),
    ):
        index = jnp.where(live, index_ref[...], -1)
        atoms = pick.shape[0] // len(classes)
        atom = lax.broadcasted_iota(jnp.int32, (atoms, edges), 0)
        for place, slots in enumerate(classes):
            hit = functools.reduce(
                jnp.logical_or, [index == atom + slot * atoms for slot in slots]
            )
            pick[place * atoms : (place + 1) * atoms, :] = jnp.where(hit, 1.0, 0.0).astype(pick.dtype)

    def copy_row(k, carry):
        spread[k] = jnp.broadcast_to(wigner[k], spread.shape[1:])
        return carry

    lax.fori_loop(0, spread.shape[0], copy_row, 0, unroll=5)
    gate[...] = radial[...].astype(jnp.float32).T
    zero_t[...] = zero[...].T
    for ref, out in ((one, one_t), (two, two_t)):
        width = ref.shape[1]
        for part in range(2):
            out[:, part * width : (part + 1) * width] = ref[part].T


def side_kernel(
    pieces, kept, *refs
):
    piece_refs, refs = refs[:pieces], refs[pieces:]
    (
        from_pick, to_pick, spread, gate, zero_t, one_t, two_t, keep, send,
        source, turned, low_zero, low_one, low_two, mixed, message,
    ) = refs
    channels, edges = gate.shape
    row = 0
    for ref in piece_refs:
        rows = ref.shape[0]
        source[row : row + rows, :] = ref[...]
        row += rows
    pick = from_pick[...]

    def gather(k, carry):
        at = pl.ds(pl.multiple_of(k * channels, channels), channels)
        turned[at, :] = lax.dot_general(
            source[:, at], pick, FIRST_FIRST, preferred_element_type=jnp.float32
        )
        return carry

    lax.fori_loop(0, COEFS, gather, 0)

    group = 16

    def forward(i, carry):
        start = i * group
        here = gate[pl.ds(pl.multiple_of(start, group), group), :]
        for degree in range(DEGREE + 1):
            within = min(degree, ORDER)
            span = 2 * degree + 1
            values = [
                turned[pl.ds(pl.multiple_of((degree * degree + c) * channels + start, group), group), :]
                for c in range(span)
            ]
            for azimuth in range(-within, within + 1):
                k = offset_of(degree, azimuth)
                total = None
                for c in range(span):
                    turn = spread[k + c]
                    term = jnp.concatenate([turn, turn], axis=0) * values[c]
                    total = term if total is None else total + term
                low = total * here
                small = low.astype(jnp.bfloat16)
                if azimuth == 0:
                    low_zero[pl.ds(pl.multiple_of(degree * channels + start, group), group), :] = small
                    continue
                order = abs(azimuth)
                ref = low_one if order == 1 else low_two
                half = ref.shape[0] // 2
                at = (degree - order) * channels + start
                first = pl.ds(pl.multiple_of(at, group), group)
                second = pl.ds(pl.multiple_of(half + at, group), group)
                if azimuth > 0:
                    ref[first, :edges] = small
                    ref[second, edges:] = small
                else:
                    ref[first, edges:] = small
                    ref[second, :edges] = (-low).astype(jnp.bfloat16)
        return carry

    lax.fori_loop(0, channels // group, forward, 0)

    mixed[: low_zero.shape[0], :] = jnp.dot(
        zero_t[...], low_zero[...], preferred_element_type=jnp.float32
    )
    base = low_zero.shape[0]
    bases = {0: 0}
    for order, table, low in ((1, one_t, low_one), (2, two_t, low_two)):
        height = table.shape[0]
        for sign in range(2):
            mixed[base : base + height, :] = jnp.dot(
                table[...], low[:, sign * edges : (sign + 1) * edges],
                preferred_element_type=jnp.float32,
            )
            bases[order if sign == 0 else -order] = base
            base += height

    def backward(i, carry):
        start = i * group
        for degree in range(DEGREE + 1):
            within = min(degree, ORDER)
            span = 2 * degree + 1
            values = {}
            for azimuth in range(-within, within + 1):
                at = bases[azimuth] + (degree - abs(azimuth)) * channels + start
                values[azimuth] = mixed[pl.ds(pl.multiple_of(at, group), group), :]
            for c in range(span):
                total = None
                for azimuth in range(-within, within + 1):
                    turn = spread[offset_of(degree, azimuth) + c]
                    term = jnp.concatenate([turn, turn], axis=0) * values[azimuth]
                    total = term if total is None else total + term
                at = (degree * degree + c) * channels + start
                message[pl.ds(pl.multiple_of(at, group), group), :] = total.astype(jnp.bfloat16)
        return carry

    lax.fori_loop(0, channels // group, backward, 0)

    spot = to_pick[...]

    def scatter(k, carry):
        at = pl.ds(pl.multiple_of(k * channels, channels), channels)
        total = lax.dot_general(spot, message[at, :], LAST_LAST, preferred_element_type=jnp.float32)
        keep[:, at] = total[:kept, :]
        send[:, at] = total[kept:, :].astype(send.dtype)
        return carry

    lax.fori_loop(0, COEFS, scatter, 0)


def one_side(pieces, from_pick, to_pick, prepared, kept, name):
    gate = prepared[1]
    channels, edges = gate.shape
    width = pieces[0].shape[1]
    slots = to_pick.shape[0]
    operands = [*pieces, from_pick, to_pick, *prepared]
    outs = (
        jax.ShapeDtypeStruct((kept, width), jnp.float32),
        jax.ShapeDtypeStruct((slots - kept, width), jnp.bfloat16),
    )
    orders = DEGREE + 1 + sum(2 * (DEGREE + 1 - m) for m in range(1, ORDER + 1))
    work = channels * edges * 2
    flops = work * (sum((DEGREE + 1 - m) ** 2 * channels * (4 if m else 1) for m in range(ORDER + 1)))
    return pl.pallas_call(
        functools.partial(side_kernel, len(pieces), kept),
        out_shape=outs,
        in_specs=[whole(o.shape) for o in operands],
        out_specs=tuple(whole(o.shape) for o in outs),
        scratch_shapes=[
            pltpu.VMEM((from_pick.shape[0], width), jnp.bfloat16),
            pltpu.VMEM((COEFS * channels, edges), jnp.float32),
            pltpu.VMEM(((DEGREE + 1) * channels, edges), jnp.bfloat16),
            pltpu.VMEM((2 * DEGREE * channels, 2 * edges), jnp.bfloat16),
            pltpu.VMEM((2 * (DEGREE - 1) * channels, 2 * edges), jnp.bfloat16),
            pltpu.VMEM((orders * channels, edges), jnp.float32),
            pltpu.VMEM((COEFS * channels, edges), jnp.bfloat16),
        ],
        compiler_params=pltpu.CompilerParams(vmem_limit_bytes=40 * 1024 * 1024),
        cost_estimate=pl.CostEstimate(flops=flops, bytes_accessed=8 << 20, transcendentals=0),
        name=name,
    )(*operands)


def prepare(edge_count, edge_tower, edge_plate, wigner, radial, zero, one, two, tower_classes, plate_classes, atoms):
    edges, channels = radial.shape
    operands = [edge_count, edge_tower, edge_plate, wigner, radial, zero, one, two]
    shape = jax.ShapeDtypeStruct
    outs = (
        shape((len(tower_classes) * atoms, edges), jnp.bfloat16),
        shape((len(plate_classes) * atoms, edges), jnp.bfloat16),
        shape((wigner.shape[0], 8, edges), jnp.float32),
        shape((channels, edges), jnp.float32),
        shape(zero.shape, jnp.bfloat16),
        shape((one.shape[1], 2 * one.shape[1]), jnp.bfloat16),
        shape((two.shape[1], 2 * two.shape[1]), jnp.bfloat16),
    )
    return pl.pallas_call(
        functools.partial(prepare_kernel, tower_classes, plate_classes),
        out_shape=outs,
        in_specs=[pl.BlockSpec(memory_space=pltpu.SMEM)] + [whole(o.shape) for o in operands[1:]],
        out_specs=tuple(whole(o.shape) for o in outs),
        compiler_params=pltpu.CompilerParams(vmem_limit_bytes=24 * 1024 * 1024),
        cost_estimate=pl.CostEstimate(flops=1 << 20, bytes_accessed=8 << 20, transcendentals=0),
        name="prepare",
    )(*operands)


def body(
    features,
    box_atoms,
    edge_count,
    edge_tower,
    edge_plate,
    wigner,
    radial,
    so2_zero,
    so2_one,
    so2_two,
):
    atoms = features.shape[3]
    width = features.shape[4]
    edges = edge_tower.shape[3]
    own = features.reshape(atoms, width)
    x_steps, y_steps, z_steps = steps_of("gx"), steps_of("gy"), steps_of("gz")
    tower_place = place_of("gx")
    tower_classes = [[s for s in range(3) if tower_place[s] == p] for p in range(len(x_steps))]
    y_place, z_place = place_of("gy"), place_of("gz")
    plate_classes = [
        [3 * e + f for e in range(3) for f in range(3) if (y_place[e], z_place[f]) == (py, pz)]
        for py in range(len(y_steps))
        for pz in range(len(z_steps))
    ]

    tower_pick, plate_pick, *prepared = prepare(
        edge_count.reshape(1),
        edge_tower.reshape(1, edges),
        edge_plate.reshape(1, edges),
        wigner.reshape(wigner.shape[3], 1, edges),
        radial.reshape(edges, radial.shape[4]),
        so2_zero,
        so2_one,
        so2_two,
        tower_classes,
        plate_classes,
        atoms,
    )

    column = jnp.concatenate([own] + [hand_on(own, "gy", -step) for step in y_steps[1:]])
    tower = [own] + [hand_on(own, "gx", -step) for step in x_steps[1:]]
    columns = [column] + [hand_on(column, "gz", -step) for step in z_steps[1:]]

    kept, sent = one_side(tower, tower_pick, plate_pick, prepared, len(z_steps) * atoms, "to_plate")
    along_y = kept
    for place, step in enumerate(y_steps[1:]):
        part = sent[place * kept.shape[0] : (place + 1) * kept.shape[0]]
        along_y = along_y + hand_on(part, "gy", step)
    plate_total = along_y[:atoms]
    for place, step in enumerate(z_steps[1:], 1):
        part = along_y[place * atoms : (place + 1) * atoms].astype(jnp.bfloat16)
        plate_total = plate_total + hand_on(part, "gz", step)

    plate = [c[place * atoms : (place + 1) * atoms] for place in range(len(y_steps)) for c in columns]
    kept, sent = one_side(plate, plate_pick, tower_pick, prepared, atoms, "to_tower")
    gathered = kept
    for place, step in enumerate(x_steps[1:]):
        gathered = gathered + hand_on(sent[place * atoms : (place + 1) * atoms], "gx", step)
    updated = own.astype(jnp.float32) + (gathered + plate_total)
    present = jnp.arange(atoms, dtype=jnp.int32) < box_atoms.reshape(())
    return jnp.where(present[:, None], updated, 0.0).astype(jnp.bfloat16).reshape(features.shape)


def solution(mesh):
    boxes = P("gx", "gy", "gz")
    placed = (
        P("gx", "gy", "gz", None, None),
        boxes,
        boxes,
        P("gx", "gy", "gz", None),
        P("gx", "gy", "gz", None),
        P("gx", "gy", "gz", None, None),
        P("gx", "gy", "gz", None, None),
        P(),
        P(),
        P(),
    )
    return jax.shard_map(
        body, mesh=mesh, in_specs=placed, out_specs=P("gx", "gy", "gz", None, None), check_vma=False
    )
```

```python
import functools

import jax
import jax.numpy as jnp
from jax import lax
from jax.experimental import pallas as pl
from jax.experimental.pallas import tpu as pltpu
from jax.sharding import PartitionSpec as P


DEGREE = 4
ORDER = 2
COEFS = (DEGREE + 1) ** 2
LAST_LAST = (((1,), (1,)), ((), ()))


def steps_of(axis):
    return (0, 1, -1)[: min(lax.axis_size(axis), 3)]


def place_of(axis):
    return [(0, 0, 0), (1, 0, 1), (2, 0, 1)][min(lax.axis_size(axis), 3) - 1]


def hand_on(block, axis, distance):
    count = lax.axis_size(axis)
    return lax.ppermute(block, axis, [(i, (i + distance) % count) for i in range(count)])


def entries():
    found = []
    for degree in range(DEGREE + 1):
        within = min(degree, ORDER)
        for azimuth in range(-within, within + 1):
            found += [(degree, azimuth, column) for column in range(2 * degree + 1)]
    return found


def offset_of(degree, azimuth):
    return entries().index((degree, azimuth, 0))


def whole(shape):
    return pl.BlockSpec(shape, lambda: (0,) * len(shape), memory_space=pltpu.VMEM)


def prepare_kernel(
    tower_classes, plate_classes, opened, count, present, tower_ref, plate_ref, features, wigner, radial, zero, one, two,
    tower_pick, plate_pick, mask, own, spread, gate, zero_t, one_t, two_t,
    count_here, present_here, wigner_here, radial_here, zero_here, one_here, two_here, arrived,
):
    loads = [
        pltpu.make_async_copy(there, here, arrived.at[place])
        for place, (there, here) in enumerate(
            (
                (count, count_here),
                (present, present_here),
                (features, own),
                (wigner, wigner_here),
                (radial, radial_here),
                (zero, zero_here),
                (one, one_here),
                (two, two_here),
            )
        )
    ]
    for load in loads:
        load.start()
    edges = radial.shape[0]
    loads[0].wait()
    loads[1].wait()
    live = lax.broadcasted_iota(jnp.int32, (1, edges), 1) < count_here[...]
    row = lax.broadcasted_iota(jnp.int32, mask.shape, 0)
    mask[...] = jnp.where(row < present_here[...], 1.0, 0.0)
    for index_ref, classes, pick in (
        (tower_ref, tower_classes, tower_pick),
        (plate_ref, plate_classes, plate_pick),
    ):
        index = jnp.where(live, index_ref[...], -1)
        atoms = pick.shape[0] // len(classes)
        atom = lax.broadcasted_iota(jnp.int32, (atoms, edges), 0)
        for place, slots in enumerate(classes):
            hit = functools.reduce(
                jnp.logical_or, [index == atom + slot * atoms for slot in slots]
            )
            pick[place * atoms : (place + 1) * atoms, :] = jnp.where(hit, 1.0, 0.0).astype(pick.dtype)

    def copy_row(k, carry):
        spread[k] = jnp.broadcast_to(wigner_here[k], spread.shape[1:])
        return carry

    loads[2].wait()
    loads[3].wait()
    lax.fori_loop(0, spread.shape[0], copy_row, 0, unroll=5)
    loads[4].wait()
    gate[...] = radial_here[...].astype(jnp.float32).T
    loads[5].wait()
    zero_t[...] = zero_here[...].T
    for load, ref, out in ((loads[6], one_here, one_t), (loads[7], two_here, two_t)):
        load.wait()
        width = ref.shape[1]
        for part in range(2):
            out[:, part * width : (part + 1) * width] = ref[part].T


GROUP = 16


def rows(at):
    return pl.ds(pl.multiple_of(at, GROUP), GROUP)


def side_kernel(pieces, shares, *refs):
    piece_refs, refs = refs[:pieces], refs[pieces:]
    from_pick, to_pick, spread, gate, zero_t, one_t, two_t, *refs = refs
    outs, refs = refs[: len(shares)], refs[len(shares) :]
    source, even, odd, low_zero, low_one, low_two, mixed, message = refs
    channels, edges = gate.shape
    lanes = 128
    for k in range(COEFS):
        at = slice(k * channels, (k + 1) * channels)
        block = jnp.concatenate([ref[:, at] for ref in piece_refs], axis=0)
        source[at, :] = block.T

    def gather(i, out):
        picked = jnp.concatenate([source[rows(k * channels + i * GROUP), :] for k in range(COEFS)], axis=0)
        out[...] = jnp.dot(picked, from_pick[...], preferred_element_type=jnp.float32)

    def forward(i, turned):
        start = i * GROUP
        for piece in range(edges // lanes):
            here_lanes = slice(piece * lanes, (piece + 1) * lanes)
            far_lanes = slice(edges + piece * lanes, edges + (piece + 1) * lanes)
            here = gate[rows(start), here_lanes]
            for degree in range(DEGREE + 1):
                within = min(degree, ORDER)
                span = 2 * degree + 1
                first_coef = degree * degree
                values = [
                    turned[(first_coef + c) * GROUP : (first_coef + c + 1) * GROUP, here_lanes]
                    for c in range(span)
                ]
                for azimuth in range(-within, within + 1):
                    k = offset_of(degree, azimuth)
                    total = None
                    for c in range(span):
                        turn = spread[k + c, :, here_lanes]
                        term = jnp.concatenate([turn, turn], axis=0) * values[c]
                        total = term if total is None else total + term
                    low = total * here
                    small = low.astype(jnp.bfloat16)
                    if azimuth == 0:
                        low_zero[rows(degree * channels + start), here_lanes] = small
                        continue
                    order = abs(azimuth)
                    ref = low_one if order == 1 else low_two
                    at = (degree - order) * channels + start
                    first, second = rows(at), rows(ref.shape[0] // 2 + at)
                    if azimuth > 0:
                        ref[first, here_lanes] = small
                        ref[second, far_lanes] = small
                    else:
                        ref[first, far_lanes] = small
                        ref[second, here_lanes] = -small

    groups = channels // GROUP
    gather(0, even)

    def pair(j, carry):
        gather(2 * j + 1, odd)
        forward(2 * j, even)
        gather(jnp.minimum(2 * j + 2, groups - 1), even)
        forward(2 * j + 1, odd)
        return carry

    lax.fori_loop(0, groups // 2, pair, 0)

    mixed[: low_zero.shape[0], :] = jnp.dot(
        zero_t[...], low_zero[...], preferred_element_type=jnp.float32
    )
    base = low_zero.shape[0]
    bases = {0: 0}
    for order, table, low in ((1, one_t, low_one), (2, two_t, low_two)):
        height = table.shape[0]
        for sign in range(2):
            mixed[base : base + height, :] = jnp.dot(
                table[...], low[:, sign * edges : (sign + 1) * edges],
                preferred_element_type=jnp.float32,
            )
            bases[order if sign == 0 else -order] = base
            base += height

    def backward(i, carry):
        start = i * GROUP
        for piece in range(edges // lanes):
            here_lanes = slice(piece * lanes, (piece + 1) * lanes)
            for degree in range(DEGREE + 1):
                within = min(degree, ORDER)
                span = 2 * degree + 1
                values = {}
                for azimuth in range(-within, within + 1):
                    at = bases[azimuth] + (degree - abs(azimuth)) * channels + start
                    values[azimuth] = mixed[rows(at), here_lanes]
                for c in range(span):
                    total = None
                    for azimuth in range(-within, within + 1):
                        turn = spread[offset_of(degree, azimuth) + c, :, here_lanes]
                        term = jnp.concatenate([turn, turn], axis=0) * values[azimuth]
                        total = term if total is None else total + term
                    at = (degree * degree + c) * channels + start
                    message[rows(at), here_lanes] = total.astype(jnp.bfloat16)
        return carry

    lax.fori_loop(0, groups, backward, 0)

    spot = to_pick[...]
    step = 5 * channels
    for at in range(0, COEFS * channels, step):
        total = lax.dot_general(
            spot, message[at : at + step, :], LAST_LAST, preferred_element_type=jnp.float32
        )
        for out, share in zip(outs, shares):
            atoms = out.shape[0] // len(share)
            for place, box in enumerate(share):
                out[place * atoms : (place + 1) * atoms, at : at + step] = total[
                    box * atoms : (box + 1) * atoms, :
                ].astype(out.dtype)


def one_side(pieces, from_pick, to_pick, prepared, shares, atoms):
    gate = prepared[1]
    channels, edges = gate.shape
    width = pieces[0].shape[1]
    operands = [*pieces, from_pick, to_pick, *prepared]
    outs = tuple(jax.ShapeDtypeStruct((len(boxes) * atoms, width), dtype) for boxes, dtype in shares)
    orders = DEGREE + 1 + sum(2 * (DEGREE + 1 - m) for m in range(1, ORDER + 1))
    work = channels * edges * 2
    flops = work * (sum((DEGREE + 1 - m) ** 2 * channels * (4 if m else 1) for m in range(ORDER + 1)))
    return pl.pallas_call(
        functools.partial(side_kernel, len(pieces), [boxes for boxes, dtype in shares]),
        out_shape=outs,
        in_specs=[whole(o.shape) for o in operands],
        out_specs=tuple(whole(o.shape) for o in outs),
        scratch_shapes=[
            pltpu.VMEM((width, from_pick.shape[0]), jnp.bfloat16),
            pltpu.VMEM((COEFS * GROUP, edges), jnp.float32),
            pltpu.VMEM((COEFS * GROUP, edges), jnp.float32),
            pltpu.VMEM(((DEGREE + 1) * channels, edges), jnp.bfloat16),
            pltpu.VMEM((2 * DEGREE * channels, 2 * edges), jnp.bfloat16),
            pltpu.VMEM((2 * (DEGREE - 1) * channels, 2 * edges), jnp.bfloat16),
            pltpu.VMEM((orders * channels, edges), jnp.float32),
            pltpu.VMEM((COEFS * channels, edges), jnp.bfloat16),
        ],
        compiler_params=pltpu.CompilerParams(vmem_limit_bytes=40 * 1024 * 1024),
        cost_estimate=pl.CostEstimate(flops=flops, bytes_accessed=8 << 20, transcendentals=0),
    )(*operands)


def opening_kernel(out):
    out[...] = jnp.zeros_like(out)


def opening():
    return pl.pallas_call(
        opening_kernel,
        out_shape=jax.ShapeDtypeStruct((8, 128), jnp.float32),
        out_specs=whole((8, 128)),
        compiler_params=pltpu.CompilerParams(vmem_limit_bytes=1024 * 1024),
        cost_estimate=pl.CostEstimate(flops=20000000000, bytes_accessed=4096, transcendentals=0),
        name="opening",
    )()


def prepare(
    edge_count, box_atoms, edge_tower, edge_plate, own, wigner, radial, zero, one, two, tower_classes, plate_classes
):
    edges, channels = radial.shape
    atoms = own.shape[0]
    shape = jax.ShapeDtypeStruct
    opened = opening()
    operands = [edge_count, box_atoms, edge_tower, edge_plate, own, wigner, radial, zero, one, two]
    outs = (
        shape((len(tower_classes) * atoms, edges), jnp.bfloat16),
        shape((len(plate_classes) * atoms, edges), jnp.bfloat16),
        shape((atoms, 128), jnp.float32),
        shape(own.shape, own.dtype),
        shape((wigner.shape[0], 8, edges), jnp.float32),
        shape((channels, edges), jnp.float32),
        shape(zero.shape, jnp.bfloat16),
        shape((one.shape[1], 2 * one.shape[1]), jnp.bfloat16),
        shape((two.shape[1], 2 * two.shape[1]), jnp.bfloat16),
    )
    there = pl.BlockSpec(memory_space=pltpu.HBM)
    return pl.pallas_call(
        functools.partial(prepare_kernel, tower_classes, plate_classes),
        out_shape=outs,
        in_specs=[whole(opened.shape)] + [there] * 2 + [whole(o.shape) for o in operands[2:4]] + [there] * 6,
        out_specs=tuple(whole(o.shape) for o in outs),
        scratch_shapes=[pltpu.VMEM(o.shape, o.dtype) for o in operands[:2] + operands[5:]]
        + [pltpu.SemaphoreType.DMA((8,))],
        compiler_params=pltpu.CompilerParams(vmem_limit_bytes=24 * 1024 * 1024),
        cost_estimate=pl.CostEstimate(flops=1 << 20, bytes_accessed=8 << 20, transcendentals=0),
        name="prepare",
    )(opened, *operands)


def body(
    features,
    box_atoms,
    edge_count,
    edge_tower,
    edge_plate,
    wigner,
    radial,
    so2_zero,
    so2_one,
    so2_two,
):
    atoms = features.shape[3]
    width = features.shape[4]
    edges = edge_tower.shape[3]
    start = features.reshape(atoms, width)
    x_steps, y_steps, z_steps = steps_of("gx"), steps_of("gy"), steps_of("gz")
    x_place, y_place, z_place = place_of("gx"), place_of("gy"), place_of("gz")
    tower_classes = [[s for s in range(3) if x_place[s] == p] for p in range(len(x_steps))]
    plate_classes = [
        [3 * e + f for e in range(3) for f in range(3) if (y_place[e], z_place[f]) == (py, pz)]
        for pz in range(len(z_steps))
        for py in range(len(y_steps))
    ]

    beside = [hand_on(start, "gy", -step) for step in y_steps[1:]]
    tower = [hand_on(start, "gx", -step) for step in x_steps[1:]]
    tower_pick, plate_pick, mask, own, *prepared = prepare(
        edge_count.reshape(1, 1),
        box_atoms.reshape(1, 1),
        edge_tower.reshape(1, edges),
        edge_plate.reshape(1, edges),
        start,
        wigner.reshape(wigner.shape[3], 1, edges),
        radial.reshape(edges, radial.shape[4]),
        so2_zero,
        so2_one,
        so2_two,
        tower_classes,
        plate_classes,
    )
    column = jnp.concatenate([own] + beside)
    columns = [hand_on(column, "gz", -step) for step in z_steps[1:]]

    across = len(y_steps)
    ends = range(1, len(z_steps))
    here = [([pz * across], jnp.float32) for pz in range(len(z_steps))]
    there = [
        share
        for py in range(1, across)
        for share in (([pz * across + py for pz in ends], jnp.bfloat16), ([py], jnp.bfloat16))
    ]
    sums = one_side([own] + tower, tower_pick, plate_pick, prepared, here + there, atoms)
    kept, leaving = sums[: len(here)], sums[len(here) :]
    kept = list(kept)
    for p, step in enumerate(y_steps[1:]):
        side = hand_on(leaving[2 * p], "gy", step)
        middle = hand_on(leaving[2 * p + 1], "gy", step)
        kept[0] = kept[0] + middle
        for pz in ends:
            kept[pz] = kept[pz] + side[(pz - 1) * atoms : pz * atoms]
    plate_total = kept[0]
    for p, step in enumerate(z_steps[1:]):
        plate_total = plate_total + hand_on(kept[p + 1].astype(jnp.bfloat16), "gz", step)

    shares = [([0], jnp.float32)] + [([p], jnp.bfloat16) for p in range(1, len(x_steps))]
    gathered, *leaving = one_side([own] + beside + columns, plate_pick, tower_pick, prepared, shares, atoms)
    for p, step in enumerate(x_steps[1:]):
        gathered = gathered + hand_on(leaving[p], "gx", step)
    updated = own.astype(jnp.float32) + (gathered + plate_total)
    return jnp.where(mask[:, :1] > 0, updated, 0.0).astype(jnp.bfloat16).reshape(features.shape)


def solution(mesh):
    boxes = P("gx", "gy", "gz")
    placed = (
        P("gx", "gy", "gz", None, None),
        boxes,
        boxes,
        P("gx", "gy", "gz", None),
        P("gx", "gy", "gz", None),
        P("gx", "gy", "gz", None, None),
        P("gx", "gy", "gz", None, None),
        P(),
        P(),
        P(),
    )

    return jax.shard_map(body, mesh=mesh, in_specs=placed, out_specs=P("gx", "gy", "gz", None, None), check_vma=False)
```

```python
import functools

import jax
import jax.numpy as jnp
from jax import lax
from jax.experimental import pallas as pl
from jax.experimental.pallas import tpu as pltpu
from jax.sharding import PartitionSpec as P


DEGREE = 4
ORDER = 2
COEFS = (DEGREE + 1) ** 2
LAST_LAST = (((1,), (1,)), ((), ()))


def steps_of(axis):
    return (0, 1, -1)[: min(lax.axis_size(axis), 3)]


def place_of(axis):
    return [(0, 0, 0), (1, 0, 1), (2, 0, 1)][min(lax.axis_size(axis), 3) - 1]


def hand_on(block, axis, distance):
    count = lax.axis_size(axis)
    return lax.ppermute(block, axis, [(i, (i + distance) % count) for i in range(count)])


def entries():
    found = []
    for degree in range(DEGREE + 1):
        within = min(degree, ORDER)
        for azimuth in range(-within, within + 1):
            found += [(degree, azimuth, column) for column in range(2 * degree + 1)]
    return found


def offset_of(degree, azimuth):
    return entries().index((degree, azimuth, 0))


def whole(shape):
    return pl.BlockSpec(shape, lambda: (0,) * len(shape), memory_space=pltpu.VMEM)


def prepare_kernel(
    tower_classes, plate_classes, opened, tower_ref, plate_ref, features, wigner, radial, zero, one, two,
    tower_pick, plate_pick, own, spread, gate, zero_t, one_t, two_t,
):
    edges = radial.shape[0]
    for index_ref, classes, pick in (
        (tower_ref, tower_classes, tower_pick),
        (plate_ref, plate_classes, plate_pick),
    ):
        index = index_ref[...]
        atoms = pick.shape[0] // len(classes)
        atom = lax.broadcasted_iota(jnp.int32, (atoms, edges), 0)
        for place, slots in enumerate(classes):
            hit = functools.reduce(
                jnp.logical_or, [index == atom + slot * atoms for slot in slots]
            )
            pick[place * atoms : (place + 1) * atoms, :] = jnp.where(hit, 1.0, 0.0).astype(pick.dtype)

    def copy_row(k, carry):
        spread[k] = jnp.broadcast_to(wigner[k], spread.shape[1:])
        return carry

    lax.fori_loop(0, spread.shape[0], copy_row, 0, unroll=5)
    own[...] = features[...]
    gate[...] = radial[...].astype(jnp.float32).T
    zero_t[...] = zero[...].T
    for ref, out in ((one, one_t), (two, two_t)):
        width = ref.shape[1]
        for part in range(2):
            out[:, part * width : (part + 1) * width] = ref[part].T


GROUP = 16


def rows(at):
    return slice(at, at + GROUP) if isinstance(at, int) else pl.ds(pl.multiple_of(at, GROUP), GROUP)


def side_kernel(pieces, shares, count, *refs):
    piece_refs, refs = refs[:pieces], refs[pieces:]
    from_pick, to_pick, spread, gate, zero_t, one_t, two_t, *refs = refs
    outs, refs = refs[: len(shares)], refs[len(shares) :]
    source, turned, low_zero, low_one, low_two, message, *mixed = refs
    mixed = dict(zip((0, *range(1, ORDER + 1), *range(-ORDER, 0)), mixed))
    channels, edges = gate.shape
    lanes = 128

    def gather(degree):
        first, last = degree * degree, (degree + 1) ** 2
        for k in range(first, last):
            at = slice(k * channels, (k + 1) * channels)
            source[at, :] = jnp.concatenate([ref[:, at] for ref in piece_refs], axis=0).T
        at = slice(first * channels, last * channels)
        turned[at, :] = jnp.dot(source[at, :], from_pick[...], preferred_element_type=jnp.float32)

    def spans():
        return [slice(piece * lanes, (piece + 1) * lanes) for piece in range(edges // lanes)]

    def turn(k, at):
        row = spread[k, :, at]
        return jnp.concatenate([row, row], axis=0)

    def forward(start, azimuth):
        order = abs(azimuth)
        for at in spans():
            far = slice(edges + at.start, edges + at.stop)
            here = gate[rows(start), at]
            for degree in range(order, DEGREE + 1):
                k = offset_of(degree, azimuth)
                total = None
                for c in range(2 * degree + 1):
                    term = turn(k + c, at) * turned[rows((degree * degree + c) * channels + start), at]
                    total = term if total is None else total + term
                small = (total * here).astype(jnp.bfloat16)
                place = (degree - order) * channels + start
                if azimuth == 0:
                    low_zero[rows(place), at] = small
                    continue
                ref = low_one if order == 1 else low_two
                first, second = rows(place), rows(ref.shape[0] // 2 + place)
                if azimuth > 0:
                    ref[first, at] = small
                    ref[second, far] = small
                else:
                    ref[first, far] = small
                    ref[second, at] = -small

    def backward(start, degree):
        within = min(degree, ORDER)
        for at in spans():
            values = {
                azimuth: mixed[azimuth][rows((degree - abs(azimuth)) * channels + start), at]
                for azimuth in range(-within, within + 1)
            }
            for c in range(2 * degree + 1):
                total = None
                for azimuth, value in values.items():
                    term = turn(offset_of(degree, azimuth) + c, at) * value
                    total = term if total is None else total + term
                message[rows((degree * degree + c) * channels + start), at] = total.astype(jnp.bfloat16)

    def product(order):
        if order == 0:
            mixed[0][...] = jnp.dot(zero_t[...], low_zero[...], preferred_element_type=jnp.float32)
            return
        table, low = (one_t, low_one) if order == 1 else (two_t, low_two)
        for azimuth, at in ((order, slice(0, edges)), (-order, slice(edges, 2 * edges))):
            mixed[azimuth][...] = jnp.dot(table[...], low[:, at], preferred_element_type=jnp.float32)

    def scatter(degree):
        at = slice(degree * degree * channels, (degree + 1) ** 2 * channels)
        total = lax.dot_general(spot, message[at, :], LAST_LAST, preferred_element_type=jnp.float32)
        for out, share in zip(outs, shares):
            atoms = out.shape[0] // len(share)
            for place, box in enumerate(share):
                out[place * atoms : (place + 1) * atoms, at] = total[
                    box * atoms : (box + 1) * atoms, :
                ].astype(out.dtype)

    starts = range(0, channels, GROUP)
    for degree in range(DEGREE + 1):
        gather(degree)

    def first_order(i, carry):
        forward(i * GROUP, 0)
        return carry

    lax.fori_loop(0, channels // GROUP, first_order, 0)
    live = lax.broadcasted_iota(jnp.int32, to_pick.shape, 1) < count[0]
    spot = jnp.where(live, to_pick[...].astype(jnp.float32), 0.0).astype(jnp.bfloat16)
    for order in range(1, ORDER + 1):
        product(order - 1)
        for start in starts:
            forward(start, order)
            forward(start, -order)
    product(ORDER)
    for degree in range(DEGREE + 1):
        for start in starts:
            backward(start, degree)
        if degree:
            scatter(degree - 1)
    scatter(DEGREE)


def one_side(count, pieces, from_pick, to_pick, prepared, shares, atoms):
    gate = prepared[1]
    channels, edges = gate.shape
    width = pieces[0].shape[1]
    operands = [*pieces, from_pick, to_pick, *prepared]
    outs = tuple(jax.ShapeDtypeStruct((len(boxes) * atoms, width), dtype) for boxes, dtype in shares)
    work = channels * edges * 2
    flops = work * (sum((DEGREE + 1 - m) ** 2 * channels * (4 if m else 1) for m in range(ORDER + 1)))
    return pl.pallas_call(
        functools.partial(side_kernel, len(pieces), [boxes for boxes, dtype in shares]),
        out_shape=outs,
        in_specs=[pl.BlockSpec(memory_space=pltpu.SMEM)] + [whole(o.shape) for o in operands],
        out_specs=tuple(whole(o.shape) for o in outs),
        scratch_shapes=[
            pltpu.VMEM((width, from_pick.shape[0]), jnp.bfloat16),
            pltpu.VMEM((COEFS * channels, edges), jnp.float32),
            pltpu.VMEM(((DEGREE + 1) * channels, edges), jnp.bfloat16),
            pltpu.VMEM((2 * DEGREE * channels, 2 * edges), jnp.bfloat16),
            pltpu.VMEM((2 * (DEGREE - 1) * channels, 2 * edges), jnp.bfloat16),
            pltpu.VMEM((COEFS * channels, edges), jnp.bfloat16),
        ]
        + [
            pltpu.VMEM(((DEGREE + 1 - abs(m)) * channels, edges), jnp.float32)
            for m in (0, *range(1, ORDER + 1), *range(-ORDER, 0))
        ],
        compiler_params=pltpu.CompilerParams(vmem_limit_bytes=40 * 1024 * 1024),
        cost_estimate=pl.CostEstimate(flops=flops, bytes_accessed=8 << 20, transcendentals=0),
    )(count, *operands)


def opening_kernel(out):
    out[...] = jnp.zeros_like(out)


def opening():
    return pl.pallas_call(
        opening_kernel,
        out_shape=jax.ShapeDtypeStruct((8, 128), jnp.float32),
        out_specs=whole((8, 128)),
        compiler_params=pltpu.CompilerParams(vmem_limit_bytes=1024 * 1024),
        cost_estimate=pl.CostEstimate(flops=20000000000, bytes_accessed=4096, transcendentals=0),
        name="opening",
    )()


def prepare(
    edge_tower, edge_plate, own, wigner, radial, zero, one, two, tower_classes, plate_classes
):
    edges, channels = radial.shape
    atoms = own.shape[0]
    shape = jax.ShapeDtypeStruct
    opened = opening()
    operands = [edge_tower, edge_plate, own, wigner, radial, zero, one, two]
    outs = (
        shape((len(tower_classes) * atoms, edges), jnp.bfloat16),
        shape((len(plate_classes) * atoms, edges), jnp.bfloat16),
        shape(own.shape, own.dtype),
        shape((wigner.shape[0], 8, edges), jnp.float32),
        shape((channels, edges), jnp.float32),
        shape(zero.shape, jnp.bfloat16),
        shape((one.shape[1], 2 * one.shape[1]), jnp.bfloat16),
        shape((two.shape[1], 2 * two.shape[1]), jnp.bfloat16),
    )
    return pl.pallas_call(
        functools.partial(prepare_kernel, tower_classes, plate_classes),
        out_shape=outs,
        in_specs=[whole(o.shape) for o in [opened] + operands],
        out_specs=tuple(whole(o.shape) for o in outs),
        compiler_params=pltpu.CompilerParams(vmem_limit_bytes=24 * 1024 * 1024),
        cost_estimate=pl.CostEstimate(flops=1 << 20, bytes_accessed=8 << 20, transcendentals=0),
        name="prepare",
    )(opened, *operands)


def body(
    features,
    box_atoms,
    edge_count,
    edge_tower,
    edge_plate,
    wigner,
    radial,
    so2_zero,
    so2_one,
    so2_two,
):
    atoms = features.shape[3]
    width = features.shape[4]
    edges = edge_tower.shape[3]
    start = features.reshape(atoms, width)
    x_steps, y_steps, z_steps = steps_of("gx"), steps_of("gy"), steps_of("gz")
    x_place, y_place, z_place = place_of("gx"), place_of("gy"), place_of("gz")
    tower_classes = [[s for s in range(3) if x_place[s] == p] for p in range(len(x_steps))]
    plate_classes = [
        [3 * e + f for e in range(3) for f in range(3) if (y_place[e], z_place[f]) == (py, pz)]
        for pz in range(len(z_steps))
        for py in range(len(y_steps))
    ]

    beside = [hand_on(start, "gy", -step) for step in y_steps[1:]]
    tower = [hand_on(start, "gx", -step) for step in x_steps[1:]]
    tower_pick, plate_pick, own, *prepared = prepare(
        edge_tower.reshape(1, edges),
        edge_plate.reshape(1, edges),
        start,
        wigner.reshape(wigner.shape[3], 1, edges),
        radial.reshape(edges, radial.shape[4]),
        so2_zero,
        so2_one,
        so2_two,
        tower_classes,
        plate_classes,
    )
    column = jnp.concatenate([start] + beside)
    columns = [hand_on(column, "gz", -step) for step in z_steps[1:]]

    count = edge_count.reshape(1)
    across = len(y_steps)
    ends = range(1, len(z_steps))
    here = [([pz * across], jnp.float32) for pz in range(len(z_steps))]
    there = [
        share
        for py in range(1, across)
        for share in (([pz * across + py for pz in ends], jnp.bfloat16), ([py], jnp.bfloat16))
    ]
    sums = one_side(count, [own] + tower, tower_pick, plate_pick, prepared, here + there, atoms)
    kept, leaving = sums[: len(here)], sums[len(here) :]
    kept = list(kept)
    middles = []
    for p, step in enumerate(y_steps[1:]):
        side = hand_on(leaving[2 * p], "gy", step)
        middle = hand_on(leaving[2 * p + 1], "gy", step)
        middles.append(middle)
        for pz in ends:
            kept[pz] = kept[pz] + side[(pz - 1) * atoms : pz * atoms]
    plate_total = functools.reduce(jnp.add, middles, kept[0])
    for p, step in enumerate(z_steps[1:]):
        plate_total = plate_total + hand_on(kept[p + 1].astype(jnp.bfloat16), "gz", step)

    shares = [([0], jnp.float32)] + [([p], jnp.bfloat16) for p in range(1, len(x_steps))]
    gathered, *leaving = one_side(count, [own] + beside + columns, plate_pick, tower_pick, prepared, shares, atoms)
    for p, step in enumerate(x_steps[1:]):
        gathered = gathered + hand_on(leaving[p], "gx", step)
    updated = own.astype(jnp.float32) + (gathered + plate_total)
    present = jnp.arange(atoms, dtype=jnp.int32) < box_atoms.reshape(())
    return jnp.where(present[:, None], updated, 0.0).astype(jnp.bfloat16).reshape(features.shape)


def solution(mesh):
    boxes = P("gx", "gy", "gz")
    placed = (
        P("gx", "gy", "gz", None, None),
        boxes,
        boxes,
        P("gx", "gy", "gz", None),
        P("gx", "gy", "gz", None),
        P("gx", "gy", "gz", None, None),
        P("gx", "gy", "gz", None, None),
        P(),
        P(),
        P(),
    )

    return jax.shard_map(body, mesh=mesh, in_specs=placed, out_specs=P("gx", "gy", "gz", None, None), check_vma=False)
```

```python
import functools

import jax
import jax.numpy as jnp
from jax import lax
from jax.experimental import pallas as pl
from jax.experimental.pallas import tpu as pltpu
from jax.sharding import PartitionSpec as P


DEGREE = 4
ORDER = 2
COEFS = (DEGREE + 1) ** 2
LAST_LAST = (((1,), (1,)), ((), ()))


def steps_of(axis):
    return (0, 1, -1)[: min(lax.axis_size(axis), 3)]


def place_of(axis):
    return [(0, 0, 0), (1, 0, 1), (2, 0, 1)][min(lax.axis_size(axis), 3) - 1]


def hand_on(block, axis, distance):
    count = lax.axis_size(axis)
    return lax.ppermute(block, axis, [(i, (i + distance) % count) for i in range(count)])


def entries():
    found = []
    for degree in range(DEGREE + 1):
        within = min(degree, ORDER)
        for azimuth in range(-within, within + 1):
            found += [(degree, azimuth, column) for column in range(2 * degree + 1)]
    return found


def offset_of(degree, azimuth):
    return entries().index((degree, azimuth, 0))


def whole(shape):
    return pl.BlockSpec(shape, lambda: (0,) * len(shape), memory_space=pltpu.VMEM)


def prepare_kernel(
    opened, features, wigner, radial, zero, one, two,
    own, spread, gate, zero_t, one_t, two_t,
):
    def copy_row(k, carry):
        spread[k] = jnp.broadcast_to(wigner[k], spread.shape[1:])
        return carry

    lax.fori_loop(0, spread.shape[0], copy_row, 0, unroll=5)
    own[...] = features[...]
    gate[...] = radial[...].astype(jnp.float32).T
    zero_t[...] = zero[...].T
    for ref, out in ((one, one_t), (two, two_t)):
        width = ref.shape[1]
        for part in range(2):
            out[:, part * width : (part + 1) * width] = ref[part].T


GROUP = 16


def rows(at):
    return slice(at, at + GROUP) if isinstance(at, int) else pl.ds(pl.multiple_of(at, GROUP), GROUP)


def side_kernel(pieces, shares, features_too, from_classes, to_classes, count, present, *refs):
    piece_refs, refs = refs[:pieces], refs[pieces:]
    from_index, to_index, spread, gate, zero_t, one_t, two_t, *refs = refs
    outs, refs = refs[: len(shares)], refs[len(shares) :]
    from_pick, to_pick, source, turned, low_zero, low_one, low_two, message, *mixed = refs
    mixed = dict(zip((0, *range(1, ORDER + 1), *range(-ORDER, 0)), mixed))
    channels, edges = gate.shape
    lanes = 128
    live = lax.broadcasted_iota(jnp.int32, (1, edges), 1) < count[0]
    for index, classes, pick in (
        (from_index[...], from_classes, from_pick),
        (jnp.where(live, to_index[...], -1), to_classes, to_pick),
    ):
        atoms = pick.shape[0] // len(classes)
        atom = lax.broadcasted_iota(jnp.int32, (atoms, edges), 0)
        for place, slots in enumerate(classes):
            hit = functools.reduce(jnp.logical_or, [index == atom + slot * atoms for slot in slots])
            pick[place * atoms : (place + 1) * atoms, :] = jnp.where(hit, 1.0, 0.0).astype(pick.dtype)

    def gather(degree):
        first, last = degree * degree, (degree + 1) ** 2
        for k in range(first, last):
            at = slice(k * channels, (k + 1) * channels)
            source[at, :] = jnp.concatenate([ref[:, at] for ref in piece_refs], axis=0).T
        at = slice(first * channels, last * channels)
        turned[at, :] = jnp.dot(source[at, :], from_pick[...], preferred_element_type=jnp.float32)

    def spans():
        return [slice(piece * lanes, (piece + 1) * lanes) for piece in range(edges // lanes)]

    def turn(k, at):
        row = spread[k, :, at]
        return jnp.concatenate([row, row], axis=0)

    def forward(start, azimuth):
        order = abs(azimuth)
        for at in spans():
            far = slice(edges + at.start, edges + at.stop)
            here = gate[rows(start), at]
            for degree in range(order, DEGREE + 1):
                k = offset_of(degree, azimuth)
                total = None
                for c in range(2 * degree + 1):
                    term = turn(k + c, at) * turned[rows((degree * degree + c) * channels + start), at]
                    total = term if total is None else total + term
                small = (total * here).astype(jnp.bfloat16)
                place = (degree - order) * channels + start
                if azimuth == 0:
                    low_zero[rows(place), at] = small
                    continue
                ref = low_one if order == 1 else low_two
                first, second = rows(place), rows(ref.shape[0] // 2 + place)
                if azimuth > 0:
                    ref[first, at] = small
                    ref[second, far] = small
                else:
                    ref[first, far] = small
                    ref[second, at] = -small

    def backward(start, degree):
        within = min(degree, ORDER)
        for at in spans():
            values = {
                azimuth: mixed[azimuth][rows((degree - abs(azimuth)) * channels + start), at]
                for azimuth in range(-within, within + 1)
            }
            for c in range(2 * degree + 1):
                total = None
                for azimuth, value in values.items():
                    term = turn(offset_of(degree, azimuth) + c, at) * value
                    total = term if total is None else total + term
                message[rows((degree * degree + c) * channels + start), at] = total.astype(jnp.bfloat16)

    def product(order):
        if order == 0:
            mixed[0][...] = jnp.dot(zero_t[...], low_zero[...], preferred_element_type=jnp.float32)
            return
        table, low = (one_t, low_one) if order == 1 else (two_t, low_two)
        for azimuth, at in ((order, slice(0, edges)), (-order, slice(edges, 2 * edges))):
            mixed[azimuth][...] = jnp.dot(table[...], low[:, at], preferred_element_type=jnp.float32)

    def scatter(degree):
        at = slice(degree * degree * channels, (degree + 1) ** 2 * channels)
        total = lax.dot_general(spot, message[at, :], LAST_LAST, preferred_element_type=jnp.float32)
        for out, share in zip(outs, shares):
            atoms = out.shape[0] // len(share)
            for place, box in enumerate(share):
                summed = total[box * atoms : (box + 1) * atoms, :]
                if features_too and out is outs[0]:
                    here = lax.broadcasted_iota(jnp.int32, summed.shape, 0) < present[0]
                    summed = summed + jnp.where(here, piece_refs[0][:, at].astype(jnp.float32), 0.0)
                out[place * atoms : (place + 1) * atoms, at] = summed.astype(out.dtype)

    starts = range(0, channels, GROUP)
    for degree in range(DEGREE + 1):
        gather(degree)

    def first_order(i, carry):
        forward(i * GROUP, 0)
        return carry

    lax.fori_loop(0, channels // GROUP, first_order, 0)
    spot = to_pick[...]
    for order in range(1, ORDER + 1):
        product(order - 1)
        for start in starts:
            forward(start, order)
            forward(start, -order)
    product(ORDER)
    for degree in range(DEGREE + 1):
        for start in starts:
            backward(start, degree)
        if degree:
            scatter(degree - 1)
    scatter(DEGREE)


def one_side(counts, pieces, from_ends, to_ends, prepared, shares, features_too, atoms):
    gate = prepared[1]
    channels, edges = gate.shape
    width = pieces[0].shape[1]
    (from_index, from_classes), (to_index, to_classes) = from_ends, to_ends
    operands = [*pieces, from_index, to_index, *prepared]
    outs = tuple(jax.ShapeDtypeStruct((len(boxes) * atoms, width), dtype) for boxes, dtype in shares)
    work = channels * edges * 2
    flops = work * (sum((DEGREE + 1 - m) ** 2 * channels * (4 if m else 1) for m in range(ORDER + 1)))
    return pl.pallas_call(
        functools.partial(
            side_kernel, len(pieces), [boxes for boxes, dtype in shares], features_too, from_classes, to_classes
        ),
        out_shape=outs,
        in_specs=[pl.BlockSpec(memory_space=pltpu.SMEM)] * 2 + [whole(o.shape) for o in operands],
        out_specs=tuple(whole(o.shape) for o in outs),
        scratch_shapes=[
            pltpu.VMEM((len(from_classes) * atoms, edges), jnp.bfloat16),
            pltpu.VMEM((len(to_classes) * atoms, edges), jnp.bfloat16),
            pltpu.VMEM((width, len(from_classes) * atoms), jnp.bfloat16),
            pltpu.VMEM((COEFS * channels, edges), jnp.float32),
            pltpu.VMEM(((DEGREE + 1) * channels, edges), jnp.bfloat16),
            pltpu.VMEM((2 * DEGREE * channels, 2 * edges), jnp.bfloat16),
            pltpu.VMEM((2 * (DEGREE - 1) * channels, 2 * edges), jnp.bfloat16),
            pltpu.VMEM((COEFS * channels, edges), jnp.bfloat16),
        ]
        + [
            pltpu.VMEM(((DEGREE + 1 - abs(m)) * channels, edges), jnp.float32)
            for m in (0, *range(1, ORDER + 1), *range(-ORDER, 0))
        ],
        compiler_params=pltpu.CompilerParams(vmem_limit_bytes=40 * 1024 * 1024),
        cost_estimate=pl.CostEstimate(flops=flops, bytes_accessed=8 << 20, transcendentals=0),
    )(*counts, *operands)


def opening_kernel(out):
    out[...] = jnp.zeros_like(out)


def opening():
    return pl.pallas_call(
        opening_kernel,
        out_shape=jax.ShapeDtypeStruct((8, 128), jnp.float32),
        out_specs=whole((8, 128)),
        compiler_params=pltpu.CompilerParams(vmem_limit_bytes=1024 * 1024),
        cost_estimate=pl.CostEstimate(flops=20000000000, bytes_accessed=4096, transcendentals=0),
        name="opening",
    )()


def prepare(own, wigner, radial, zero, one, two):
    edges, channels = radial.shape
    shape = jax.ShapeDtypeStruct
    opened = opening()
    operands = [own, wigner, radial, zero, one, two]
    outs = (
        shape(own.shape, own.dtype),
        shape((wigner.shape[0], 8, edges), jnp.float32),
        shape((channels, edges), jnp.float32),
        shape(zero.shape, jnp.bfloat16),
        shape((one.shape[1], 2 * one.shape[1]), jnp.bfloat16),
        shape((two.shape[1], 2 * two.shape[1]), jnp.bfloat16),
    )
    return pl.pallas_call(
        prepare_kernel,
        out_shape=outs,
        in_specs=[whole(o.shape) for o in [opened] + operands],
        out_specs=tuple(whole(o.shape) for o in outs),
        compiler_params=pltpu.CompilerParams(vmem_limit_bytes=24 * 1024 * 1024),
        cost_estimate=pl.CostEstimate(flops=1 << 20, bytes_accessed=8 << 20, transcendentals=0),
        name="prepare",
    )(opened, *operands)


def body(
    features,
    box_atoms,
    edge_count,
    edge_tower,
    edge_plate,
    wigner,
    radial,
    so2_zero,
    so2_one,
    so2_two,
):
    atoms = features.shape[3]
    width = features.shape[4]
    edges = edge_tower.shape[3]
    start = features.reshape(atoms, width)
    x_steps, y_steps, z_steps = steps_of("gx"), steps_of("gy"), steps_of("gz")
    x_place, y_place, z_place = place_of("gx"), place_of("gy"), place_of("gz")
    tower_classes = [[s for s in range(3) if x_place[s] == p] for p in range(len(x_steps))]
    plate_classes = [
        [3 * e + f for e in range(3) for f in range(3) if (y_place[e], z_place[f]) == (py, pz)]
        for pz in range(len(z_steps))
        for py in range(len(y_steps))
    ]

    beside = [hand_on(start, "gy", -step) for step in y_steps[1:]]
    tower = [hand_on(start, "gx", -step) for step in x_steps[1:]]
    own, *prepared = prepare(
        start,
        wigner.reshape(wigner.shape[3], 1, edges),
        radial.reshape(edges, radial.shape[4]),
        so2_zero,
        so2_one,
        so2_two,
    )
    tower_ends = (edge_tower.reshape(1, edges), tower_classes)
    plate_ends = (edge_plate.reshape(1, edges), plate_classes)
    column = jnp.concatenate([start] + beside)
    columns = [hand_on(column, "gz", -step) for step in z_steps[1:]]

    counts = (edge_count.reshape(1), box_atoms.reshape(1))
    across = len(y_steps)
    ends = range(1, len(z_steps))
    here = [([pz * across], jnp.float32) for pz in range(len(z_steps))]
    there = [
        share
        for py in range(1, across)
        for share in (([pz * across + py for pz in ends], jnp.bfloat16), ([py], jnp.bfloat16))
    ]
    sums = one_side(counts, [own] + tower, tower_ends, plate_ends, prepared, here + there, True, atoms)
    kept, leaving = sums[: len(here)], sums[len(here) :]
    kept = list(kept)
    middles = []
    for p, step in enumerate(y_steps[1:]):
        side = hand_on(leaving[2 * p], "gy", step)
        middle = hand_on(leaving[2 * p + 1], "gy", step)
        middles.append(middle)
        for pz in ends:
            kept[pz] = kept[pz] + side[(pz - 1) * atoms : pz * atoms]
    plate_total = functools.reduce(jnp.add, middles, kept[0])
    for p, step in enumerate(z_steps[1:]):
        plate_total = plate_total + hand_on(kept[p + 1].astype(jnp.bfloat16), "gz", step)

    shares = [([0], jnp.float32)] + [([p], jnp.bfloat16) for p in range(1, len(x_steps))]
    gathered, *leaving = one_side(
        counts, [own] + beside + columns, plate_ends, tower_ends, prepared, shares, False, atoms
    )
    for p, step in enumerate(x_steps[1:]):
        gathered = gathered + hand_on(leaving[p], "gx", step)
    return (gathered + plate_total).astype(jnp.bfloat16).reshape(features.shape)


def solution(mesh):
    boxes = P("gx", "gy", "gz")
    placed = (
        P("gx", "gy", "gz", None, None),
        boxes,
        boxes,
        P("gx", "gy", "gz", None),
        P("gx", "gy", "gz", None),
        P("gx", "gy", "gz", None, None),
        P("gx", "gy", "gz", None, None),
        P(),
        P(),
        P(),
    )

    return jax.shard_map(body, mesh=mesh, in_specs=placed, out_specs=P("gx", "gy", "gz", None, None), check_vma=False)
```
